32 devices in a mesh: dom: 4 (over y, x), sep: 8 (over z, core).
Axes of the slice: x: 2, y: 2, z: 4, core: 2. Of those that a mesh axis runs over, the one named last changes fastest.
Arguments:
- rhs_leaf: bfloat16 [4, 4096, 1536], P('dom', 'sep'), may hold values from -6 to 6
- rhs_middle: bfloat16 [4, 4096, 768], P('dom', 'sep'), may hold values from -6 to 6
- rhs_top: bfloat16 [4, 4096, 384], P('dom', 'sep'), may hold values from -6 to 6
- update_leaf: bfloat16 [4, 4096, 256], P('dom', 'sep'), may hold values from -0.375 to 0.375
- couple_leaf: bfloat16 [4, 4096, 256], P('dom', 'sep'), may hold values from -0.09375 to 0.09375
- update_middle: bfloat16 [4, 4096, 256], P('dom', 'sep'), may hold values from -0.375 to 0.375, as said below
- couple_middle: bfloat16 [4, 4096, 256], P('dom', 'sep'), may hold values from -0.09375 to 0.09375, as said below
- pivot_leaf: float32 [4, 4096], P('dom', 'sep'), may hold values from 2.2 to 4
- pivot_middle: float32 [2, 4096], P(None, 'sep'), may hold values from 2.2 to 4
- pivot_top: float32 [1, 4096], P(None, 'sep'), may hold values from 2.2 to 4
- front_rows: int32 [4, 8], P('dom', 'sep'), may hold values from 128 to 512, as said below
- rank_leaf: int32 [4], P('dom'), may hold values from 64 to 256, as said below
- rank_middle: int32 [2], replicated, may hold values from 64 to 256, as said below
Outputs:
- top_values: float32 [4, 4096, 384], P('dom', 'sep')
The draws below stay inside these ranges and needn't reach their ends.
Inputs may be any that keep to these rules, and one draw needn't show every extreme that they name: `front_rows`: in every draw some front has all 512 rows of some row block live. `rank_leaf`: some leaf front has rank 256 in every draw. `rank_middle`: some middle front has rank 256 in every draw. `update_middle`: rows 2g and 2g+1 are equal; entries lie within plus or minus 6 / sqrt(256). `couple_middle`: rows 2g and 2g+1 are equal; entries lie within plus or minus 6 / sqrt(4096).
All inputs are finite; a program needn't handle non-finite values.
Results may differ from the reference program's by a relative error of at most 0.0018.
Values may be sent and summed in bfloat16 or wider, within the bound.
A program may use at most 64 MiB of HBM per device.

```python
import math
import jax
import jax.numpy as jnp
from jax import lax

ROWS = 512
SRC = 1536
RANK = 256
SEP = 4096
FRONTS = 4


def paired_factor(key, salt, fan_in):
    base_key = jax.random.fold_in(key, salt)
    base = jax.random.normal(base_key, (FRONTS // 2, SEP, RANK), jnp.float32)
    scaled = jnp.clip(base, -6.0, 6.0) * fan_in ** (-0.5)
    return jnp.repeat(scaled, 2, axis=0).astype(jnp.bfloat16)


def forced_ints(key, count, lowest, highest):
    first_key, second_key = jax.random.split(key)
    values = jax.random.randint(first_key, (count,), lowest, highest + 1, jnp.int32)
    target = jax.random.randint(second_key, (), 0, count, jnp.int32)
    return jnp.where(jnp.arange(count, dtype=jnp.int32) == target, jnp.int32(highest), values)


def draw_update_middle(key, part):
    return paired_factor(key, 11, RANK)


def draw_couple_middle(key, part):
    return paired_factor(key, 23, SEP)


def draw_front_rows(key, part):
    blocks = SEP // ROWS
    values = forced_ints(jax.random.fold_in(key, 31), FRONTS * blocks, max(1, ROWS // 4), ROWS)
    return values.reshape(FRONTS, blocks)


def draw_rank_leaf(key, part):
    return forced_ints(jax.random.fold_in(key, 41), FRONTS, max(1, RANK // 4), RANK)


def draw_rank_middle(key, part):
    return forced_ints(jax.random.fold_in(key, 53), FRONTS // 2, max(1, RANK // 4), RANK)


def block_levels(stream_key, shape, cuts, low, high):
    loudness = 1.0
    for axis_at, blocks in cuts:
        steps = jax.random.uniform(jax.random.fold_in(jax.random.fold_in(stream_key, 6), axis_at), (blocks,), jnp.float32, low / len(cuts), high / len(cuts))
        loudness = loudness * jnp.repeat(jnp.exp(steps), shape[axis_at] // blocks).reshape((-1,) + (1,) * (len(shape) - 1 - axis_at))
    return loudness


def centred(own_key, dims, width, most, shards=(), held_as=jnp.bfloat16):
    entries = jax.random.normal(own_key, dims, jnp.float32) * width
    if len(shards) > 0:
        entries = block_levels(own_key, dims, shards, -0.22, 0.18) * entries
    return jnp.clip(entries, min=-most, max=most).astype(held_as)


def setup_inputs(seed: int = 0) -> dict:
    splits = jax.random.split(jax.random.key(seed), 14)
    rhs_leaf = centred(splits[0], (FRONTS, SEP, SRC), 1.0, 6.0, ((0, 4), (1, 8)))
    rhs_middle = centred(splits[1], (FRONTS, SEP, SRC // 2), 1.0, 6.0, ((0, 4), (1, 8)))
    rhs_top = centred(splits[2], (FRONTS, SEP, SRC // 4), 1.0, 6.0, ((0, 4), (1, 8)))
    update_leaf = centred(splits[3], (FRONTS, SEP, RANK), RANK ** -0.5, 0.375, ((0, 4), (1, 8)))
    couple_leaf = centred(splits[4], (FRONTS, SEP, RANK), SEP ** -0.5, 0.09375, ((0, 4), (1, 8)))
    update_middle = draw_update_middle(jax.random.fold_in(splits[13], 71), 0)
    couple_middle = draw_couple_middle(jax.random.fold_in(splits[13], 71), 0)
    pivot_leaf = jnp.clip(jnp.exp(math.log(4.0) - 0.597837 * jax.random.uniform(splits[7], (FRONTS, SEP), jnp.float32) ** block_levels(splits[7], (FRONTS, SEP), ((0, 4), (1, 8)), -0.2, 0.2)), 2.2, 4.0)
    pivot_middle = jnp.clip(jnp.exp(math.log(4.0) - 0.597837 * jax.random.uniform(splits[8], (FRONTS // 2, SEP), jnp.float32) ** block_levels(splits[8], (FRONTS // 2, SEP), ((1, 8),), -0.2, 0.2)), 2.2, 4.0)
    pivot_top = jnp.clip(jnp.exp(math.log(4.0) - 0.597837 * jax.random.uniform(splits[9], (FRONTS // 4, SEP), jnp.float32) ** block_levels(splits[9], (FRONTS // 4, SEP), ((1, 8),), -0.2, 0.2)), 2.2, 4.0)
    front_rows = draw_front_rows(jax.random.fold_in(splits[13], 71), 0)
    rank_leaf = draw_rank_leaf(jax.random.fold_in(splits[13], 71), 0)
    rank_middle = draw_rank_middle(jax.random.fold_in(splits[13], 71), 0)
    return dict(rhs_leaf=rhs_leaf, rhs_middle=rhs_middle, rhs_top=rhs_top, update_leaf=update_leaf, couple_leaf=couple_leaf, update_middle=update_middle, couple_middle=couple_middle, pivot_leaf=pivot_leaf, pivot_middle=pivot_middle, pivot_top=pivot_top, front_rows=front_rows, rank_leaf=rank_leaf, rank_middle=rank_middle)


def sep_solve(right_side, pivots, row_mask):
    scaled = row_mask[:, None] * right_side / pivots[:, None]
    zero_row = jnp.zeros((1, right_side.shape[1]), scaled.dtype)
    beside = jnp.concatenate([zero_row, scaled[:-1]], 0) + jnp.concatenate([scaled[1:], zero_row], 0)
    return scaled + row_mask[:, None] * beside / pivots[:, None]


def coupling(factor, values, rank):
    partial_sum = lax.dot_general(factor, values, (((0,), (0,)), ((), ())), preferred_element_type=jnp.float32)
    rank_keep = (jnp.arange(RANK) < rank).astype(jnp.float32)
    return (partial_sum * rank_keep[:, None]).astype(jnp.bfloat16)


def reference(rhs_leaf, rhs_middle, rhs_top, update_leaf, couple_leaf, update_middle, couple_middle, pivot_leaf, pivot_middle, pivot_top, front_rows, rank_leaf, rank_middle):
    half_width = SRC // 2
    quarter = SRC // 4
    row_ids = jnp.arange(SEP)
    local_row = row_ids % ROWS
    row_block = row_ids // ROWS
    every_row = jnp.ones((SEP,), jnp.float32)

    def level_one(g):
        coefficient_list = []
        for child in (0, 1):
            leaf = 2 * g + child
            live = (local_row < front_rows[leaf][row_block]).astype(jnp.float32)
            values = sep_solve(rhs_leaf[leaf].astype(jnp.float32), pivot_leaf[leaf], live).astype(jnp.bfloat16)
            coefficient_list.append(coupling(couple_leaf[leaf], values, rank_leaf[leaf]))
        halves = []
        for side in (0, 1):
            running = rhs_middle[2 * g + side].astype(jnp.float32)
            for child in (0, 1):
                running = running - jnp.dot(update_leaf[2 * g + child], coefficient_list[child][:, side * half_width:(side + 1) * half_width], preferred_element_type=jnp.float32)
            halves.append(running)
        middle_rhs = jnp.concatenate(halves, 1)
        middle_values = sep_solve(middle_rhs, pivot_middle[g], every_row).astype(jnp.bfloat16)
        return coupling(couple_middle[2 * g], middle_values, rank_middle[g])

    middle_coef = lax.map(level_one, jnp.arange(FRONTS // 2, dtype=jnp.int32))

    def level_two(q):
        results = []
        for j in range(4):
            front = 4 * q + j
            column_start = (j % 2) * half_width + (j // 2) * quarter
            running = rhs_top[front].astype(jnp.float32)
            for child in (0, 1):
                middle = 2 * q + child
                running = running - jnp.dot(update_middle[2 * middle], middle_coef[middle][:, column_start:column_start + quarter], preferred_element_type=jnp.float32)
            results.append(sep_solve(running, pivot_top[q], every_row))
        return jnp.stack(results)

    top_values = lax.map(level_two, jnp.arange(FRONTS // 4, dtype=jnp.int32))
    return top_values.reshape(FRONTS, SEP, quarter)
```

```python
import functools

import jax
import jax.numpy as jnp
from jax import lax
from jax.experimental import pallas as pl
from jax.experimental.pallas import tpu as pltpu
from jax.sharding import PartitionSpec as P

MESH = pl.DeviceIdType.MESH
F32 = jnp.float32
BF16 = jnp.bfloat16
CW = 128
HOP = 3
LAG = 2
LAND = 2


def flipped(value, bit):
    return value + bit - 2 * bit * (lax.rem(value // bit, 2))


def spread(row, height):
    return jnp.broadcast_to(row, (height, row.shape[1])).T


def kernel(
    n_sep,
    rhs_leaf, rhs_middle, rhs_top, update_leaf, couple_leaf, update_middle, couple_middle,
    pivot_leaf, pivot_middle, pivot_top, front_rows, rank_leaf, rank_middle,
    out,
    leaf_v, middle_v, top_v, couple_v, factor_leaf, factor_middle,
    turned_leaf, turned_middle, weights,
    edge_send, edge_recv, row_send, row_recv,
    pair_send, pair_recv, own, leaf_lines, middle_lines, final_send,
    coef_leaf, coef_middle,
    load_sem, factor_send_sem, factor_recv_sem, edge_send_sem, edge_recv_sem,
    row_send_sem, row_recv_sem,
    pair_send_sem, pair_recv_sem, right_send_sem, left_send_sem, right_recv_sem, left_recv_sem,
    final_send_sem, coef_leaf_sem, coef_middle_sem,
):
    front = lax.axis_index("dom")
    sep = lax.axis_index("sep")
    n_z = n_sep // 2
    z = sep // 2
    core = lax.rem(sep, 2)
    side = lax.rem(front, 2)
    group = lax.rem(front // 2, 2)
    across = flipped(front, 1)
    over = flipped(front, 2)
    sibling = flipped(sep, 1)
    beside = sep - 1 + 2 * core
    has_beside = jnp.logical_and(beside >= 0, beside < n_sep)
    n_beside = has_beside.astype(jnp.int32)
    not_first = (z > 0).astype(jnp.int32)
    not_last = (z < n_z - 1).astype(jnp.int32)

    rows, width = leaf_v.shape
    half = width // 2
    quarter = width // 4
    rank = couple_v.shape[2]
    own_rank = rank // 2
    n_top = quarter // CW
    n_mid = 2 * n_top
    n_leaf = 2 * n_mid

    loads = [
        pltpu.make_async_copy(rhs_leaf.at[0], leaf_v, load_sem.at[0]),
        pltpu.make_async_copy(couple_leaf.at[0], couple_v.at[0], load_sem.at[1]),
        pltpu.make_async_copy(
            update_leaf.at[0], factor_leaf.at[side, pl.ds(0, rows)], load_sem.at[2]
        ),
        pltpu.make_async_copy(
            update_middle.at[0], factor_middle.at[group, pl.ds(0, rows)], load_sem.at[3]
        ),
        pltpu.make_async_copy(rhs_middle.at[0], middle_v, load_sem.at[4]),
        pltpu.make_async_copy(rhs_top.at[0], top_v, load_sem.at[5]),
        pltpu.make_async_copy(couple_middle.at[0], couple_v.at[1], load_sem.at[6]),
    ]
    for load in loads:
        load.start()

    barrier = pltpu.get_barrier_semaphore()

    def greet(dom_at, sep_at):
        pl.semaphore_signal(barrier, inc=1, device_id=(dom_at, sep_at), device_id_type=MESH)

    for dom_at in (front, across, over):
        greet(dom_at, sibling)
    for dom_at in (across, over):
        greet(dom_at, sep)

    @pl.when(has_beside)
    def _():
        for dom_at in (front, across, over):
            greet(dom_at, beside)

    @pl.when(z > 0)
    def _():
        greet(front, sep - 2)

    @pl.when(z < n_z - 1)
    def _():
        greet(front, sep + 2)

    @pl.when(sep == 0)
    def _():
        edge_recv[0] = jnp.zeros(edge_recv.shape[1:], F32)
        for slot in range(3):
            row_recv[slot, 0] = jnp.zeros(row_recv.shape[2:], F32)

    @pl.when(sep == n_sep - 1)
    def _():
        edge_recv[1] = jnp.zeros(edge_recv.shape[1:], F32)
        for slot in range(3):
            row_recv[slot, 1] = jnp.zeros(row_recv.shape[2:], F32)

    @pl.when(z == 0)
    def _():
        for lines in (leaf_lines, middle_lines):
            lines[2] = jnp.zeros(lines.shape[1:], lines.dtype)

    @pl.when(z == n_z - 1)
    def _():
        for lines in (leaf_lines, middle_lines):
            lines[3] = jnp.zeros(lines.shape[1:], lines.dtype)

    row_at = lax.broadcasted_iota(jnp.int32, (rows, CW), 0)
    live = (row_at < front_rows[0, 0]).astype(F32)
    weights[0] = live * (1.0 / spread(pivot_leaf[...], CW))
    weights[1] = 1.0 / spread(pivot_middle[pl.ds(front // 2, 1), :], CW)
    weights[2] = 1.0 / spread(pivot_top[pl.ds(front // 4, 1), :], CW)

    for load in loads[:6]:
        load.wait()

    ends = (rows - 16, 0)
    picks = (15, 0)
    for way in range(2):
        block = pl.ds(ends[way], 16)
        pick = slice(picks[way], picks[way] + 1)
        leaf_row = leaf_v[block, :].astype(F32)[pick]
        leaf_weight = weights[0, block, :][pick][:, :1]
        edge_send[way, :, :width] = leaf_row * leaf_weight
        edge_send[way, :, width : width + half] = middle_v[block, :].astype(F32)[pick]
        edge_send[way, :, width + half : width + half + quarter] = (
            top_v[block, :].astype(F32)[pick]
        )
        tail = width + half + quarter
        edge_send[way, :, tail : tail + CW] = weights[1, block, :][pick]
        edge_send[way, :, tail + CW : tail + 2 * CW] = weights[2, block, :][pick]
        row_send[way, :, :rank] = factor_leaf[side, block, :].astype(F32)[pick]
        row_send[way, :, rank:] = factor_middle[group, block, :].astype(F32)[pick]

    pl.semaphore_wait(barrier, 5 + 3 * n_beside + not_first + not_last)

    def edge_copies(way, target):
        copies = [
            pltpu.make_async_remote_copy(
                edge_send.at[way], edge_recv.at[way], edge_send_sem.at[way],
                edge_recv_sem.at[way], device_id=(front, target), device_id_type=MESH,
            )
        ]
        for slot, dom_at in enumerate((front, across, over)):
            copies.append(
                pltpu.make_async_remote_copy(
                    row_send.at[way], row_recv.at[slot, way], row_send_sem.at[slot, way],
                    row_recv_sem.at[slot, way], device_id=(dom_at, target), device_id_type=MESH,
                )
            )
        return copies

    to_next = edge_copies(0, sep + 1)
    to_prev = edge_copies(1, sep - 1)

    @pl.when(sep < n_sep - 1)
    def _():
        for copy in to_next:
            copy.start()

    @pl.when(sep > 0)
    def _():
        for copy in to_prev:
            copy.start()

    factor_copies = [
        pltpu.make_async_remote_copy(
            factor_leaf.at[side, pl.ds(0, rows)], factor_leaf.at[side, pl.ds(0, rows)],
            factor_send_sem.at[0], factor_recv_sem.at[0],
            device_id=(across, sep), device_id_type=MESH,
        ),
        pltpu.make_async_remote_copy(
            factor_middle.at[group, pl.ds(0, rows)], factor_middle.at[group, pl.ds(0, rows)],
            factor_send_sem.at[1], factor_recv_sem.at[1],
            device_id=(over, sep), device_id_type=MESH,
        ),
    ]
    for copy in factor_copies:
        copy.start()

    def turn(which, turned):
        for part in range(2):
            at = pl.multiple_of(own_rank * (core if part == 0 else 1 - core), own_rank)
            turned[pl.ds(part * own_rank, own_rank), :] = couple_v[
                which, :, pl.ds(at, own_rank)
            ].T

    turn(0, turned_leaf)

    @pl.when(sep > 0)
    def _():
        to_next[0].wait_recv()

    @pl.when(sep < n_sep - 1)
    def _():
        to_prev[0].wait_recv()

    def solved(right_side, weight, before, after):
        scaled = right_side * weight
        up = jnp.where(row_at == 0, before, pltpu.roll(scaled, 1, 0))
        down = jnp.where(row_at == rows - 1, after, pltpu.roll(scaled, rows - 1, 0))
        return scaled + weight * (up + down)

    def place(i):
        here = lax.rem(i, 2)
        at_quarter = here * group + (1 - here) * (1 - group)
        return at_quarter * n_top + i // 2

    def to_device(src, dst, send_sem, recv_sem, dom_at, sep_at):
        return pltpu.make_async_remote_copy(
            src, dst, send_sem, recv_sem, device_id=(dom_at, sep_at), device_id_type=MESH
        )

    def pair_copy(slot):
        return to_device(
            pair_send.at[slot], pair_recv.at[slot], pair_send_sem.at[slot],
            pair_recv_sem.at[slot], front, sibling,
        )

    def right_copy(lines, first_slot, j):
        slot = first_slot + j
        return to_device(
            lines.at[0, j], lines.at[2, j], right_send_sem.at[slot],
            right_recv_sem.at[slot], front, sep + 2,
        )

    def left_copy(lines, first_slot, j):
        slot = first_slot + j
        return to_device(
            lines.at[1, j], lines.at[3, j], left_send_sem.at[slot],
            left_recv_sem.at[slot], front, sep - 2,
        )

    def final_copy(slot, coef, sem, child, i, dom_at, sep_at, lane):
        return to_device(
            final_send.at[slot],
            coef.at[child, i, pl.ds(pl.multiple_of(core * own_rank, own_rank), own_rank)],
            final_send_sem.at[slot, lax.rem(lane, 2)], sem.at[i, lane], dom_at, sep_at,
        )

    def start_pair(slot, turned, values):
        part = jnp.dot(turned[...], values, preferred_element_type=F32)
        own[slot] = part[:own_rank]
        pair_send[slot] = part[own_rank:]
        pair_copy(slot).start()

    def chain(t, count, base, first_slot, stride, lines, rank_now, coef, coef_sem, child, partner):
        def on(step, body):
            j = (step + stride * count) // stride - count
            hit = jnp.logical_and(lax.rem(step + stride * count, stride) == 0, True)

            @pl.when(jnp.logical_and(hit, jnp.logical_and(step >= 0, j < count)))
            def _():
                body(j)

        def add_pair(j):
            slot = first_slot + j
            pair_copy(slot).wait_recv()
            own[slot] += pair_recv[slot]

        def prefix(j):
            slot = first_slot + j

            @pl.when(z > 0)
            def _():
                right_copy(lines, first_slot, j).wait_recv()

            @pl.when(z < n_z - 1)
            def _():
                lines[0, j] = (own[slot] + lines[2, j].astype(F32)).astype(lines.dtype)
                right_copy(lines, first_slot, j).start()

        def suffix(j):
            slot = first_slot + j

            @pl.when(z < n_z - 1)
            def _():
                left_copy(lines, first_slot, j).wait_recv()

            @pl.when(z > 0)
            def _():
                lines[1, j] = (own[slot] + lines[3, j].astype(F32)).astype(lines.dtype)
                left_copy(lines, first_slot, j).start()

        def final(j):
            slot = first_slot + j
            total = own[slot] + lines[2, j].astype(F32) + lines[3, j].astype(F32)
            at = core * own_rank + lax.broadcasted_iota(jnp.int32, total.shape, 0)
            kept = jnp.where(at < rank_now, total, 0.0).astype(BF16)
            final_send[slot] = kept
            i = j // 2

            @pl.when(lax.rem(j, 2) == 1)
            def _():
                coef[child, i, pl.ds(pl.multiple_of(core * own_rank, own_rank), own_rank)] = kept
                final_copy(slot, coef, coef_sem, child, i, front, sibling, 0).start()

            @pl.when(lax.rem(j, 2) == 0)
            def _():
                final_copy(slot, coef, coef_sem, child, i, partner, sep, 1).start()
                final_copy(slot, coef, coef_sem, child, i, partner, sibling, 2).start()

        start = t - base
        on(start, add_pair)
        on(start - z * HOP, prefix)
        on(start - (n_z - 1 - z) * HOP, suffix)
        on(start - jnp.maximum(z, n_z - 1 - z) * HOP, final)

    def await_coef(coef, sem, child, i):
        block = coef.at[child, i, pl.ds(0, own_rank)]
        for lane in range(3):
            to_device(
                final_send.at[0], block, final_send_sem.at[0, 0], sem.at[i, lane], front, sibling
            ).wait_recv()

    def applied(factor, coef, i):
        return jnp.dot(factor[0], coef[0, i], preferred_element_type=F32) + jnp.dot(
            factor[1], coef[1, i], preferred_element_type=F32
        )

    def leaf_step(j):
        i = j // 2
        own_side = lax.rem(j, 2)
        at_side = own_side * side + (1 - own_side) * (1 - side)
        at = pl.multiple_of(at_side * half + place(i) * CW, CW)
        values = solved(
            leaf_v[:, pl.ds(at, CW)].astype(F32), weights[0],
            edge_recv[0, :, pl.ds(at, CW)], edge_recv[1, :, pl.ds(at, CW)],
        ).astype(BF16)
        start_pair(j, turned_leaf, values)

    tail = width + half + quarter

    def eliminated(right_v, offset, at, factor, coef, i, which):
        taken = applied(factor, coef, i)
        beyond = []
        for way in range(2):
            right = edge_recv[way, :, pl.ds(pl.multiple_of(offset + at, CW), CW)]
            weight = edge_recv[way, :, tail + (which - 1) * CW : tail + which * CW]
            beyond.append((right - taken[rows + way : rows + way + 1]) * weight)
        return solved(
            right_v[:, pl.ds(at, CW)].astype(F32) - taken[:rows], weights[which], *beyond
        )

    def middle_step(i):
        await_coef(coef_leaf, coef_leaf_sem, side, i)
        at = pl.multiple_of(place(i) * CW, CW)
        values = eliminated(middle_v, width, at, factor_leaf, coef_leaf, i, 1).astype(BF16)
        start_pair(n_leaf + i, turned_middle, values)

    def top_step(i):
        await_coef(coef_middle, coef_middle_sem, group, i)
        at = pl.multiple_of(i * CW, CW)
        out[0, :, pl.ds(at, CW)] = eliminated(
            top_v, width + half, at, factor_middle, coef_middle, i, 2
        )

    def ready():
        loads[6].wait()
        turn(1, turned_middle)

        @pl.when(sep > 0)
        def _():
            for copy in to_next[1:]:
                copy.wait_recv()

        @pl.when(sep < n_sep - 1)
        def _():
            for copy in to_prev[1:]:
                copy.wait_recv()

        for copy in factor_copies:
            copy.wait_recv()

        at_row = lax.broadcasted_iota(jnp.int32, (16, rank), 0)

        def edge_tile(slot, lanes):
            before = row_recv[slot, 0, :, lanes]
            after = row_recv[slot, 1, :, lanes]
            tile = jnp.where(at_row == 0, before, jnp.where(at_row == 1, after, 0.0))
            return tile.astype(BF16)

        low, high = slice(0, rank), slice(rank, 2 * rank)
        factor_leaf[side, rows : rows + 16, :] = edge_tile(0, low)
        factor_leaf[1 - side, rows : rows + 16, :] = edge_tile(1, low)
        factor_middle[group, rows : rows + 16, :] = edge_tile(0, high)
        factor_middle[1 - group, rows : rows + 16, :] = edge_tile(2, high)

    leaf_base = LAG
    middle_at = leaf_base + (n_z - 1) * HOP + LAND + 1
    middle_base = middle_at + LAG
    top_at = middle_base + 2 + (n_z - 1) * HOP + LAND
    steps = top_at + 4 * (n_top - 1) + 1
    rank_leaf_now = rank_leaf[0]
    rank_middle_now = rank_middle[front // 2]

    def step(t, carry):
        @pl.when(t < n_leaf)
        def _():
            leaf_step(t)

        @pl.when(t == n_leaf)
        def _():
            ready()

        chain(
            t, n_leaf, leaf_base, 0, 1, leaf_lines, rank_leaf_now, coef_leaf, coef_leaf_sem,
            side, across,
        )

        i_mid = t - middle_at

        @pl.when(
            jnp.logical_and(i_mid >= 0, jnp.logical_and(i_mid < 2 * n_mid, lax.rem(i_mid, 2) == 0))
        )
        def _():
            middle_step(i_mid // 2)

        chain(
            t, n_mid, middle_base, n_leaf, 2, middle_lines, rank_middle_now, coef_middle, coef_middle_sem,
            group, over,
        )

        i_top = t - top_at

        @pl.when(jnp.logical_and(i_top >= 0, lax.rem(i_top, 4) == 0))
        def _():
            top_step(i_top // 4)

        return carry

    lax.fori_loop(0, steps, step, 0)

    @pl.when(sep < n_sep - 1)
    def _():
        for copy in to_next:
            copy.wait_send()

    @pl.when(sep > 0)
    def _():
        for copy in to_prev:
            copy.wait_send()

    for copy in factor_copies:
        copy.wait_send()

    def drain(lines, first_slot, j, carry):
        slot = first_slot + j
        pair_copy(slot).wait_send()

        @pl.when(z < n_z - 1)
        def _():
            right_copy(lines, first_slot, j).wait_send()

        @pl.when(z > 0)
        def _():
            left_copy(lines, first_slot, j).wait_send()

        final_copy(slot, coef_leaf, coef_leaf_sem, side, 0, front, sibling, 0).wait_send()

        @pl.when(lax.rem(j, 2) == 0)
        def _():
            final_copy(slot, coef_leaf, coef_leaf_sem, side, 0, across, sep, 1).wait_send()

        return carry

    lax.fori_loop(0, n_leaf, functools.partial(drain, leaf_lines, 0), 0)
    lax.fori_loop(0, n_mid, functools.partial(drain, middle_lines, n_leaf), 0)


def shards(*operands):
    n_sep = lax.axis_size("sep")
    rows, width = operands[0].shape[1:]
    rank = operands[3].shape[2]
    half, quarter = width // 2, width // 4
    own_rank = rank // 2
    n_top = quarter // CW
    n_mid = 2 * n_top
    slots = 3 * n_mid
    chunk = (slots, own_rank, CW)
    tail = width + half + quarter + 2 * CW
    dma = pltpu.SemaphoreType.DMA
    hbm = pl.BlockSpec(memory_space=pl.ANY)
    vmem = pl.BlockSpec(memory_space=pltpu.VMEM)
    smem = pl.BlockSpec(memory_space=pltpu.SMEM)
    return pl.pallas_call(
        functools.partial(kernel, n_sep),
        out_shape=jax.ShapeDtypeStruct((1, rows, quarter), F32),
        in_specs=[hbm] * 7 + [vmem] * 3 + [smem] * 3,
        out_specs=vmem,
        scratch_shapes=[
            pltpu.VMEM((rows, width), BF16),
            pltpu.VMEM((rows, half), BF16),
            pltpu.VMEM((rows, quarter), BF16),
            pltpu.VMEM((2, rows, rank), BF16),
            pltpu.VMEM((2, rows + 16, rank), BF16),
            pltpu.VMEM((2, rows + 16, rank), BF16),
            pltpu.VMEM((rank, rows), BF16),
            pltpu.VMEM((rank, rows), BF16),
            pltpu.VMEM((3, rows, CW), F32),
            pltpu.VMEM((2, 1, tail), F32),
            pltpu.VMEM((2, 1, tail), F32),
            pltpu.VMEM((2, 1, 2 * rank), F32),
            pltpu.VMEM((3, 2, 1, 2 * rank), F32),
            pltpu.VMEM(chunk, F32),
            pltpu.VMEM(chunk, F32),
            pltpu.VMEM(chunk, F32),
            pltpu.VMEM((4, 2 * n_mid, own_rank, CW), BF16),
            pltpu.VMEM((4, n_mid, own_rank, CW), F32),
            pltpu.VMEM(chunk, BF16),
            pltpu.VMEM((2, n_mid, rank, CW), BF16),
            pltpu.VMEM((2, n_top, rank, CW), BF16),
            dma((7,)),
            dma((2,)),
            dma((2,)),
            dma((2,)),
            dma((2,)),
            dma((3, 2)),
            dma((3, 2)),
            dma((slots,)),
            dma((slots,)),
            dma((slots,)),
            dma((slots,)),
            dma((slots,)),
            dma((slots,)),
            dma((slots, 2)),
            dma((n_mid, 3)),
            dma((n_top, 3)),
        ],
        compiler_params=pltpu.CompilerParams(
            collective_id=0, has_side_effects=True, vmem_limit_bytes=50 * 1024 * 1024
        ),
    )(*operands)


def solution(mesh):
    return jax.shard_map(
        shards,
        mesh=mesh,
        in_specs=(
            P("dom", "sep", None),
            P("dom", "sep", None),
            P("dom", "sep", None),
            P("dom", "sep", None),
            P("dom", "sep", None),
            P("dom", "sep", None),
            P("dom", "sep", None),
            P("dom", "sep"),
            P(None, "sep"),
            P(None, "sep"),
            P("dom", "sep"),
            P("dom"),
            P(),
        ),
        out_specs=P("dom", "sep", None),
        check_vma=False,
    )
```

```python
import functools

import jax
import jax.numpy as jnp
from jax import lax
from jax.experimental import pallas as pl
from jax.experimental.pallas import tpu as pltpu
from jax.sharding import PartitionSpec as P

MESH = pl.DeviceIdType.MESH
F32 = jnp.float32
BF16 = jnp.bfloat16
CW = 128
HOP = 5
LAG = 3
LAND = 4


def flipped(value, bit):
    return value + bit - 2 * bit * (lax.rem(value // bit, 2))


def spread(row, height):
    return jnp.broadcast_to(row, (height, row.shape[1])).T


def kernel(
    n_sep,
    rhs_leaf, rhs_middle, rhs_top, update_leaf, couple_leaf, update_middle, couple_middle,
    pivot_leaf, pivot_middle, pivot_top, front_rows, rank_leaf, rank_middle,
    out,
    pivot_v,
    leaf_v, middle_v, top_v, couple_v, factor_leaf, factor_middle,
    turned_leaf, turned_middle, weights,
    edge_send, edge_recv, row_send, row_recv,
    pair_send, pair_recv, own, leaf_lines, middle_lines, final_send,
    coef_leaf, coef_middle,
    load_sem, factor_send_sem, factor_recv_sem, edge_send_sem, edge_recv_sem,
    row_send_sem, row_recv_sem,
    pair_send_sem, pair_recv_sem, right_send_sem, left_send_sem, right_recv_sem, left_recv_sem,
    final_send_sem, coef_leaf_sem, coef_middle_sem,
):
    front = lax.axis_index("dom")
    sep = lax.axis_index("sep")
    n_z = n_sep // 2
    z = sep // 2
    core = lax.rem(sep, 2)
    side = lax.rem(front, 2)
    group = lax.rem(front // 2, 2)
    across = flipped(front, 1)
    over = flipped(front, 2)
    sibling = flipped(sep, 1)
    beside = sep - 1 + 2 * core
    has_beside = jnp.logical_and(beside >= 0, beside < n_sep)
    n_beside = has_beside.astype(jnp.int32)
    not_first = (z > 0).astype(jnp.int32)
    not_last = (z < n_z - 1).astype(jnp.int32)

    rows, width = leaf_v.shape
    half = width // 2
    quarter = width // 4
    rank = couple_v.shape[2]
    own_rank = rank // 2
    n_top = quarter // CW
    n_mid = 2 * n_top
    n_leaf = 2 * n_mid

    loads = [
        pltpu.make_async_copy(pivot_leaf, pivot_v.at[0], load_sem.at[7]),
        pltpu.make_async_copy(pivot_middle.at[pl.ds(front // 2, 1)], pivot_v.at[1], load_sem.at[8]),
        pltpu.make_async_copy(pivot_top.at[pl.ds(front // 4, 1)], pivot_v.at[2], load_sem.at[9]),
        pltpu.make_async_copy(rhs_leaf.at[0], leaf_v, load_sem.at[0]),
        pltpu.make_async_copy(couple_leaf.at[0], couple_v.at[0], load_sem.at[1]),
        pltpu.make_async_copy(
            update_leaf.at[0], factor_leaf.at[side, pl.ds(0, rows)], load_sem.at[2]
        ),
        pltpu.make_async_copy(
            update_middle.at[0], factor_middle.at[group, pl.ds(0, rows)], load_sem.at[3]
        ),
        pltpu.make_async_copy(rhs_middle.at[0], middle_v, load_sem.at[4]),
        pltpu.make_async_copy(rhs_top.at[0], top_v, load_sem.at[5]),
        pltpu.make_async_copy(couple_middle.at[0], couple_v.at[1], load_sem.at[6]),
    ]
    for load in loads:
        load.start()

    barrier = pltpu.get_barrier_semaphore()

    def greet(dom_at, sep_at):
        pl.semaphore_signal(barrier, inc=1, device_id=(dom_at, sep_at), device_id_type=MESH)

    for dom_at in (front, across, over):
        greet(dom_at, sibling)
    for dom_at in (across, over):
        greet(dom_at, sep)

    @pl.when(has_beside)
    def _():
        for dom_at in (front, across, over):
            greet(dom_at, beside)

    @pl.when(z > 0)
    def _():
        greet(front, sep - 2)

    @pl.when(z < n_z - 1)
    def _():
        greet(front, sep + 2)

    @pl.when(sep == 0)
    def _():
        edge_recv[0] = jnp.zeros(edge_recv.shape[1:], F32)
        for slot in range(3):
            row_recv[slot, 0] = jnp.zeros(row_recv.shape[2:], F32)

    @pl.when(sep == n_sep - 1)
    def _():
        edge_recv[1] = jnp.zeros(edge_recv.shape[1:], F32)
        for slot in range(3):
            row_recv[slot, 1] = jnp.zeros(row_recv.shape[2:], F32)

    @pl.when(z == 0)
    def _():
        for lines in (leaf_lines, middle_lines):
            lines[2] = jnp.zeros(lines.shape[1:], lines.dtype)

    @pl.when(z == n_z - 1)
    def _():
        for lines in (leaf_lines, middle_lines):
            lines[3] = jnp.zeros(lines.shape[1:], lines.dtype)

    row_at = lax.broadcasted_iota(jnp.int32, (rows, CW), 0)
    live = (row_at < front_rows[0, 0]).astype(F32)
    for load in loads[:3]:
        load.wait()
    weights[0] = live * (1.0 / spread(pivot_v[0], CW))
    weights[1] = 1.0 / spread(pivot_v[1], CW)
    weights[2] = 1.0 / spread(pivot_v[2], CW)

    for load in loads[3:9]:
        load.wait()

    ends = (rows - 16, 0)
    picks = (15, 0)
    for way in range(2):
        block = pl.ds(ends[way], 16)
        pick = slice(picks[way], picks[way] + 1)
        leaf_row = leaf_v[block, :].astype(F32)[pick]
        leaf_weight = weights[0, block, :][pick][:, :1]
        edge_send[way, :, :width] = leaf_row * leaf_weight
        edge_send[way, :, width : width + half] = middle_v[block, :].astype(F32)[pick]
        edge_send[way, :, width + half : width + half + quarter] = (
            top_v[block, :].astype(F32)[pick]
        )
        tail = width + half + quarter
        edge_send[way, :, tail : tail + CW] = weights[1, block, :][pick]
        edge_send[way, :, tail + CW : tail + 2 * CW] = weights[2, block, :][pick]
        row_send[way, :, :rank] = factor_leaf[side, block, :].astype(F32)[pick]
        row_send[way, :, rank:] = factor_middle[group, block, :].astype(F32)[pick]

    pl.semaphore_wait(barrier, 5 + 3 * n_beside + not_first + not_last)

    def edge_copies(way, target):
        copies = [
            pltpu.make_async_remote_copy(
                edge_send.at[way], edge_recv.at[way], edge_send_sem.at[way],
                edge_recv_sem.at[way], device_id=(front, target), device_id_type=MESH,
            )
        ]
        for slot, dom_at in enumerate((front, across, over)):
            copies.append(
                pltpu.make_async_remote_copy(
                    row_send.at[way], row_recv.at[slot, way], row_send_sem.at[slot, way],
                    row_recv_sem.at[slot, way], device_id=(dom_at, target), device_id_type=MESH,
                )
            )
        return copies

    to_next = edge_copies(0, sep + 1)
    to_prev = edge_copies(1, sep - 1)

    @pl.when(sep < n_sep - 1)
    def _():
        for copy in to_next:
            copy.start()

    @pl.when(sep > 0)
    def _():
        for copy in to_prev:
            copy.start()

    factor_copies = [
        pltpu.make_async_remote_copy(
            factor_leaf.at[side, pl.ds(0, rows)], factor_leaf.at[side, pl.ds(0, rows)],
            factor_send_sem.at[0], factor_recv_sem.at[0],
            device_id=(across, sep), device_id_type=MESH,
        ),
        pltpu.make_async_remote_copy(
            factor_middle.at[group, pl.ds(0, rows)], factor_middle.at[group, pl.ds(0, rows)],
            factor_send_sem.at[1], factor_recv_sem.at[1],
            device_id=(over, sep), device_id_type=MESH,
        ),
    ]
    for copy in factor_copies:
        copy.start()

    def turn(which, turned):
        for part in range(2):
            at = pl.multiple_of(own_rank * (core if part == 0 else 1 - core), own_rank)
            turned[pl.ds(part * own_rank, own_rank), :] = couple_v[
                which, :, pl.ds(at, own_rank)
            ].T

    turn(0, turned_leaf)

    @pl.when(sep > 0)
    def _():
        to_next[0].wait_recv()

    @pl.when(sep < n_sep - 1)
    def _():
        to_prev[0].wait_recv()

    def solved(right_side, weight, before, after):
        scaled = right_side * weight
        up = jnp.where(row_at == 0, before, pltpu.roll(scaled, 1, 0))
        down = jnp.where(row_at == rows - 1, after, pltpu.roll(scaled, rows - 1, 0))
        return scaled + weight * (up + down)

    def place(i):
        here = lax.rem(i, 2)
        at_quarter = here * group + (1 - here) * (1 - group)
        return at_quarter * n_top + lax.div(i, 2)

    def to_device(src, dst, send_sem, recv_sem, dom_at, sep_at):
        return pltpu.make_async_remote_copy(
            src, dst, send_sem, recv_sem, device_id=(dom_at, sep_at), device_id_type=MESH
        )

    def pair_copy(slot):
        return to_device(
            pair_send.at[slot], pair_recv.at[slot], pair_send_sem.at[slot],
            pair_recv_sem.at[slot], front, sibling,
        )

    def right_copy(lines, first_slot, j):
        slot = first_slot + j
        return to_device(
            lines.at[0, j], lines.at[2, j], right_send_sem.at[slot],
            right_recv_sem.at[slot], front, sep + 2,
        )

    def left_copy(lines, first_slot, j):
        slot = first_slot + j
        return to_device(
            lines.at[1, j], lines.at[3, j], left_send_sem.at[slot],
            left_recv_sem.at[slot], front, sep - 2,
        )

    def final_copy(slot, coef, sem, child, i, dom_at, sep_at, lane):
        return to_device(
            final_send.at[slot],
            coef.at[child, i, pl.ds(pl.multiple_of(core * own_rank, own_rank), own_rank)],
            final_send_sem.at[slot, lax.rem(lane, 2)], sem.at[i, lane], dom_at, sep_at,
        )

    def start_pair(slot, turned, values):
        part = jnp.dot(turned[...], values, preferred_element_type=F32)
        own[slot] = part[:own_rank]
        pair_send[slot] = part[own_rank:]
        pair_copy(slot).start()

    def chain(t, count, base, first_slot, stride, lines, rank_now, coef, coef_sem, child, partner):
        def on(step, body):
            j = lax.div(step, stride) if stride > 1 else step
            hit = jnp.logical_and(step >= 0, step < stride * count)
            if stride > 1:
                hit = jnp.logical_and(hit, lax.rem(step, stride) == 0)

            @pl.when(hit)
            def _():
                body(j)

        def add_pair(j):
            slot = first_slot + j
            pair_copy(slot).wait_recv()
            own[slot] += pair_recv[slot]

        def prefix(j):
            slot = first_slot + j

            @pl.when(z > 0)
            def _():
                right_copy(lines, first_slot, j).wait_recv()

            @pl.when(z < n_z - 1)
            def _():
                lines[0, j] = (own[slot] + lines[2, j].astype(F32)).astype(lines.dtype)
                right_copy(lines, first_slot, j).start()

        def suffix(j):
            slot = first_slot + j

            @pl.when(z < n_z - 1)
            def _():
                left_copy(lines, first_slot, j).wait_recv()

            @pl.when(z > 0)
            def _():
                lines[1, j] = (own[slot] + lines[3, j].astype(F32)).astype(lines.dtype)
                left_copy(lines, first_slot, j).start()

        def final(j):
            slot = first_slot + j
            total = own[slot] + lines[2, j].astype(F32) + lines[3, j].astype(F32)
            at = core * own_rank + lax.broadcasted_iota(jnp.int32, total.shape, 0)
            kept = jnp.where(at < rank_now, total, 0.0).astype(BF16)
            final_send[slot] = kept
            i = lax.div(j, 2)

            @pl.when(lax.rem(j, 2) == 1)
            def _():
                coef[child, i, pl.ds(pl.multiple_of(core * own_rank, own_rank), own_rank)] = kept
                final_copy(slot, coef, coef_sem, child, i, front, sibling, 0).start()

            @pl.when(lax.rem(j, 2) == 0)
            def _():
                final_copy(slot, coef, coef_sem, child, i, partner, sep, 1).start()
                final_copy(slot, coef, coef_sem, child, i, partner, sibling, 2).start()

        start = t - base
        on(start, add_pair)
        on(start - z * HOP, prefix)
        on(start - (n_z - 1 - z) * HOP, suffix)
        on(start - jnp.maximum(z, n_z - 1 - z) * HOP, final)

    def await_coef(coef, sem, child, i):
        block = coef.at[child, i, pl.ds(0, own_rank)]
        for lane in range(3):
            to_device(
                final_send.at[0], block, final_send_sem.at[0, 0], sem.at[i, lane], front, sibling
            ).wait_recv()

    def applied(factor, coef, i):
        return jnp.dot(factor[0], coef[0, i], preferred_element_type=F32) + jnp.dot(
            factor[1], coef[1, i], preferred_element_type=F32
        )

    def leaf_step(j):
        i = lax.div(j, 2)
        own_side = lax.rem(j, 2)
        at_side = own_side * side + (1 - own_side) * (1 - side)
        at = pl.multiple_of(at_side * half + place(i) * CW, CW)
        values = solved(
            leaf_v[:, pl.ds(at, CW)].astype(F32), weights[0],
            edge_recv[0, :, pl.ds(at, CW)], edge_recv[1, :, pl.ds(at, CW)],
        ).astype(BF16)
        start_pair(j, turned_leaf, values)

    tail = width + half + quarter

    def eliminated(right_v, offset, at, factor, coef, i, which):
        taken = applied(factor, coef, i)
        beyond = []
        for way in range(2):
            right = edge_recv[way, :, pl.ds(pl.multiple_of(offset + at, CW), CW)]
            weight = edge_recv[way, :, tail + (which - 1) * CW : tail + which * CW]
            beyond.append((right - taken[rows + way : rows + way + 1]) * weight)
        return solved(
            right_v[:, pl.ds(at, CW)].astype(F32) - taken[:rows], weights[which], *beyond
        )

    def middle_step(i):
        await_coef(coef_leaf, coef_leaf_sem, side, i)
        at = pl.multiple_of(place(i) * CW, CW)
        values = eliminated(middle_v, width, at, factor_leaf, coef_leaf, i, 1).astype(BF16)
        start_pair(n_leaf + i, turned_middle, values)

    def top_step(i):
        await_coef(coef_middle, coef_middle_sem, group, i)
        at = pl.multiple_of(i * CW, CW)
        out[0, :, pl.ds(at, CW)] = eliminated(
            top_v, width + half, at, factor_middle, coef_middle, i, 2
        )

    def ready():
        loads[9].wait()
        turn(1, turned_middle)

        @pl.when(sep > 0)
        def _():
            for copy in to_next[1:]:
                copy.wait_recv()

        @pl.when(sep < n_sep - 1)
        def _():
            for copy in to_prev[1:]:
                copy.wait_recv()

        for copy in factor_copies:
            copy.wait_recv()

        at_row = lax.broadcasted_iota(jnp.int32, (16, rank), 0)

        def edge_tile(slot, lanes):
            before = row_recv[slot, 0, :, lanes]
            after = row_recv[slot, 1, :, lanes]
            tile = jnp.where(at_row == 0, before, jnp.where(at_row == 1, after, 0.0))
            return tile.astype(BF16)

        low, high = slice(0, rank), slice(rank, 2 * rank)
        factor_leaf[side, rows : rows + 16, :] = edge_tile(0, low)
        factor_leaf[1 - side, rows : rows + 16, :] = edge_tile(1, low)
        factor_middle[group, rows : rows + 16, :] = edge_tile(0, high)
        factor_middle[1 - group, rows : rows + 16, :] = edge_tile(2, high)

    leaf_base = LAG
    middle_at = leaf_base + (n_z - 1) * HOP + LAND + 1
    middle_base = middle_at + LAG
    top_at = middle_base + 2 + (n_z - 1) * HOP + LAND
    steps = top_at + 4 * (n_top - 1) + 1
    rank_leaf_now = rank_leaf[0]
    rank_middle_now = rank_middle[front // 2]

    def step(t, carry):
        @pl.when(t < n_leaf)
        def _():
            leaf_step(t)

        @pl.when(t == n_leaf)
        def _():
            ready()

        @pl.when(t < leaf_base + n_leaf + (n_z - 1) * HOP)
        def _():
            chain(
                t, n_leaf, leaf_base, 0, 1, leaf_lines, rank_leaf_now, coef_leaf, coef_leaf_sem,
                side, across,
            )

        i_mid = t - middle_at

        @pl.when(
            jnp.logical_and(i_mid >= 0, jnp.logical_and(i_mid < 2 * n_mid, lax.rem(i_mid, 2) == 0))
        )
        def _():
            middle_step(lax.div(i_mid, 2))

        @pl.when(t >= middle_base)
        def _():
            chain(
                t, n_mid, middle_base, n_leaf, 2, middle_lines, rank_middle_now, coef_middle,
                coef_middle_sem, group, over,
            )

        i_top = t - top_at

        @pl.when(jnp.logical_and(i_top >= 0, lax.rem(i_top, 4) == 0))
        def _():
            top_step(lax.div(i_top, 4))

        return carry

    lax.fori_loop(0, steps, step, 0)

    @pl.when(sep < n_sep - 1)
    def _():
        for copy in to_next:
            copy.wait_send()

    @pl.when(sep > 0)
    def _():
        for copy in to_prev:
            copy.wait_send()

    for copy in factor_copies:
        copy.wait_send()

    def drain(lines, first_slot, j, carry):
        slot = first_slot + j
        pair_copy(slot).wait_send()

        @pl.when(z < n_z - 1)
        def _():
            right_copy(lines, first_slot, j).wait_send()

        @pl.when(z > 0)
        def _():
            left_copy(lines, first_slot, j).wait_send()

        final_copy(slot, coef_leaf, coef_leaf_sem, side, 0, front, sibling, 0).wait_send()

        @pl.when(lax.rem(j, 2) == 0)
        def _():
            final_copy(slot, coef_leaf, coef_leaf_sem, side, 0, across, sep, 1).wait_send()

        return carry

    lax.fori_loop(0, n_leaf, functools.partial(drain, leaf_lines, 0), 0)
    lax.fori_loop(0, n_mid, functools.partial(drain, middle_lines, n_leaf), 0)


def shards(*operands):
    n_sep = lax.axis_size("sep")
    rows, width = operands[0].shape[1:]
    rank = operands[3].shape[2]
    half, quarter = width // 2, width // 4
    own_rank = rank // 2
    n_top = quarter // CW
    n_mid = 2 * n_top
    slots = 3 * n_mid
    chunk = (slots, own_rank, CW)
    tail = width + half + quarter + 2 * CW
    dma = pltpu.SemaphoreType.DMA
    hbm = pl.BlockSpec(memory_space=pltpu.HBM)
    vmem = pl.BlockSpec(memory_space=pltpu.VMEM)
    smem = pl.BlockSpec(memory_space=pltpu.SMEM)
    return pl.pallas_call(
        functools.partial(kernel, n_sep),
        out_shape=jax.ShapeDtypeStruct((1, rows, quarter), F32),
        in_specs=[hbm] * 10 + [smem] * 3,
        out_specs=vmem,
        scratch_shapes=[
            pltpu.VMEM((3, 1, rows), F32),
            pltpu.VMEM((rows, width), BF16),
            pltpu.VMEM((rows, half), BF16),
            pltpu.VMEM((rows, quarter), BF16),
            pltpu.VMEM((2, rows, rank), BF16),
            pltpu.VMEM((2, rows + 16, rank), BF16),
            pltpu.VMEM((2, rows + 16, rank), BF16),
            pltpu.VMEM((rank, rows), BF16),
            pltpu.VMEM((rank, rows), BF16),
            pltpu.VMEM((3, rows, CW), F32),
            pltpu.VMEM((2, 1, tail), F32),
            pltpu.VMEM((2, 1, tail), F32),
            pltpu.VMEM((2, 1, 2 * rank), F32),
            pltpu.VMEM((3, 2, 1, 2 * rank), F32),
            pltpu.VMEM(chunk, F32),
            pltpu.VMEM(chunk, F32),
            pltpu.VMEM(chunk, F32),
            pltpu.VMEM((4, 2 * n_mid, own_rank, CW), BF16),
            pltpu.VMEM((4, n_mid, own_rank, CW), F32),
            pltpu.VMEM(chunk, BF16),
            pltpu.VMEM((2, n_mid, rank, CW), BF16),
            pltpu.VMEM((2, n_top, rank, CW), BF16),
            dma((10,)),
            dma((2,)),
            dma((2,)),
            dma((2,)),
            dma((2,)),
            dma((3, 2)),
            dma((3, 2)),
            dma((slots,)),
            dma((slots,)),
            dma((slots,)),
            dma((slots,)),
            dma((slots,)),
            dma((slots,)),
            dma((slots, 2)),
            dma((n_mid, 3)),
            dma((n_top, 3)),
        ],
        compiler_params=pltpu.CompilerParams(
            collective_id=0, has_side_effects=True, vmem_limit_bytes=67043328
        ),
    )(*operands)


def solution(mesh):
    return jax.shard_map(
        shards,
        mesh=mesh,
        in_specs=(
            P("dom", "sep", None),
            P("dom", "sep", None),
            P("dom", "sep", None),
            P("dom", "sep", None),
            P("dom", "sep", None),
            P("dom", "sep", None),
            P("dom", "sep", None),
            P("dom", "sep"),
            P(None, "sep"),
            P(None, "sep"),
            P("dom", "sep"),
            P("dom"),
            P(),
        ),
        out_specs=P("dom", "sep", None),
        check_vma=False,
    )
```

```python
import functools

import jax
import jax.numpy as jnp
from jax import lax
from jax.experimental import pallas as pl
from jax.experimental.pallas import tpu as pltpu
from jax.sharding import PartitionSpec as P

MESH = pl.DeviceIdType.MESH
F32 = jnp.float32
BF16 = jnp.bfloat16
CW = 128
HOP = 5
LAG = 3
LAND = 4


def flipped(value, bit):
    return value + bit - 2 * bit * (lax.rem(value // bit, 2))


def spread(row, height):
    return jnp.broadcast_to(row, (height, row.shape[1])).T


def kernel(
    n_sep,
    rhs_leaf, rhs_middle, rhs_top, update_leaf, couple_leaf, update_middle, couple_middle,
    pivot_leaf, pivot_middle, pivot_top, front_rows_hbm, rank_leaf_hbm, rank_middle_hbm,
    out,
    front_rows, rank_leaf, rank_middle, pivot_v,
    leaf_v, middle_v, top_v, couple_v, factor_leaf, factor_middle,
    turned_leaf, turned_middle, weights,
    edge_send, edge_recv, row_send, row_recv,
    pair_send, pair_recv, own, leaf_lines, middle_lines, final_send,
    coef_leaf, coef_middle,
    load_sem, factor_send_sem, factor_recv_sem, edge_send_sem, edge_recv_sem,
    row_send_sem, row_recv_sem,
    pair_send_sem, pair_recv_sem, right_send_sem, left_send_sem, right_recv_sem, left_recv_sem,
    final_send_sem, coef_leaf_sem, coef_middle_sem,
):
    front = lax.axis_index("dom")
    sep = lax.axis_index("sep")
    n_z = n_sep // 2
    z = sep // 2
    core = lax.rem(sep, 2)
    side = lax.rem(front, 2)
    group = lax.rem(front // 2, 2)
    across = flipped(front, 1)
    over = flipped(front, 2)
    sibling = flipped(sep, 1)
    beside = sep - 1 + 2 * core
    has_beside = jnp.logical_and(beside >= 0, beside < n_sep)
    n_beside = has_beside.astype(jnp.int32)
    not_first = (z > 0).astype(jnp.int32)
    not_last = (z < n_z - 1).astype(jnp.int32)

    rows, width = leaf_v.shape
    half = width // 2
    quarter = width // 4
    rank = couple_v.shape[2]
    own_rank = rank // 2
    n_top = quarter // CW
    n_mid = 2 * n_top
    n_leaf = 2 * n_mid

    loads = [
        pltpu.make_async_copy(front_rows_hbm, front_rows, load_sem.at[10]),
        pltpu.make_async_copy(rank_leaf_hbm, rank_leaf, load_sem.at[11]),
        pltpu.make_async_copy(rank_middle_hbm, rank_middle, load_sem.at[12]),
        pltpu.make_async_copy(pivot_leaf, pivot_v.at[0], load_sem.at[7]),
        pltpu.make_async_copy(pivot_middle.at[pl.ds(front // 2, 1)], pivot_v.at[1], load_sem.at[8]),
        pltpu.make_async_copy(pivot_top.at[pl.ds(front // 4, 1)], pivot_v.at[2], load_sem.at[9]),
        pltpu.make_async_copy(rhs_leaf.at[0], leaf_v, load_sem.at[0]),
        pltpu.make_async_copy(couple_leaf.at[0], couple_v.at[0], load_sem.at[1]),
        pltpu.make_async_copy(
            update_leaf.at[0], factor_leaf.at[side, pl.ds(0, rows)], load_sem.at[2]
        ),
        pltpu.make_async_copy(
            update_middle.at[0], factor_middle.at[group, pl.ds(0, rows)], load_sem.at[3]
        ),
        pltpu.make_async_copy(rhs_middle.at[0], middle_v, load_sem.at[4]),
        pltpu.make_async_copy(rhs_top.at[0], top_v, load_sem.at[5]),
        pltpu.make_async_copy(couple_middle.at[0], couple_v.at[1], load_sem.at[6]),
    ]
    for load in loads:
        load.start()

    barrier = pltpu.get_barrier_semaphore()

    def greet(dom_at, sep_at):
        pl.semaphore_signal(barrier, inc=1, device_id=(dom_at, sep_at), device_id_type=MESH)

    for dom_at in (front, across, over):
        greet(dom_at, sibling)
    for dom_at in (across, over):
        greet(dom_at, sep)

    @pl.when(has_beside)
    def _():
        for dom_at in (front, across, over):
            greet(dom_at, beside)

    @pl.when(z > 0)
    def _():
        greet(front, sep - 2)

    @pl.when(z < n_z - 1)
    def _():
        greet(front, sep + 2)

    @pl.when(sep == 0)
    def _():
        edge_recv[0] = jnp.zeros(edge_recv.shape[1:], F32)
        for slot in range(3):
            row_recv[slot, 0] = jnp.zeros(row_recv.shape[2:], F32)

    @pl.when(sep == n_sep - 1)
    def _():
        edge_recv[1] = jnp.zeros(edge_recv.shape[1:], F32)
        for slot in range(3):
            row_recv[slot, 1] = jnp.zeros(row_recv.shape[2:], F32)

    @pl.when(z == 0)
    def _():
        for lines in (leaf_lines, middle_lines):
            lines[2] = jnp.zeros(lines.shape[1:], lines.dtype)

    @pl.when(z == n_z - 1)
    def _():
        for lines in (leaf_lines, middle_lines):
            lines[3] = jnp.zeros(lines.shape[1:], lines.dtype)

    for load in loads[:6]:
        load.wait()
    row_at = lax.broadcasted_iota(jnp.int32, (rows, CW), 0)
    live = (row_at < front_rows[0, 0]).astype(F32)
    weights[0] = live * (1.0 / spread(pivot_v[0], CW))
    weights[1] = 1.0 / spread(pivot_v[1], CW)
    weights[2] = 1.0 / spread(pivot_v[2], CW)

    for load in loads[6:12]:
        load.wait()

    ends = (rows - 16, 0)
    picks = (15, 0)
    for way in range(2):
        block = pl.ds(ends[way], 16)
        pick = slice(picks[way], picks[way] + 1)
        leaf_row = leaf_v[block, :].astype(F32)[pick]
        leaf_weight = weights[0, block, :][pick][:, :1]
        edge_send[way, :, :width] = leaf_row * leaf_weight
        edge_send[way, :, width : width + half] = middle_v[block, :].astype(F32)[pick]
        edge_send[way, :, width + half : width + half + quarter] = (
            top_v[block, :].astype(F32)[pick]
        )
        tail = width + half + quarter
        edge_send[way, :, tail : tail + CW] = weights[1, block, :][pick]
        edge_send[way, :, tail + CW : tail + 2 * CW] = weights[2, block, :][pick]
        row_send[way, :, :rank] = factor_leaf[side, block, :].astype(F32)[pick]
        row_send[way, :, rank:] = factor_middle[group, block, :].astype(F32)[pick]

    pl.semaphore_wait(barrier, 5 + 3 * n_beside + not_first + not_last)

    def edge_copies(way, target):
        copies = [
            pltpu.make_async_remote_copy(
                edge_send.at[way], edge_recv.at[way], edge_send_sem.at[way],
                edge_recv_sem.at[way], device_id=(front, target), device_id_type=MESH,
            )
        ]
        for slot, dom_at in enumerate((front, across, over)):
            copies.append(
                pltpu.make_async_remote_copy(
                    row_send.at[way], row_recv.at[slot, way], row_send_sem.at[slot, way],
                    row_recv_sem.at[slot, way], device_id=(dom_at, target), device_id_type=MESH,
                )
            )
        return copies

    to_next = edge_copies(0, sep + 1)
    to_prev = edge_copies(1, sep - 1)

    @pl.when(sep < n_sep - 1)
    def _():
        for copy in to_next:
            copy.start()

    @pl.when(sep > 0)
    def _():
        for copy in to_prev:
            copy.start()

    factor_copies = [
        pltpu.make_async_remote_copy(
            factor_leaf.at[side, pl.ds(0, rows)], factor_leaf.at[side, pl.ds(0, rows)],
            factor_send_sem.at[0], factor_recv_sem.at[0],
            device_id=(across, sep), device_id_type=MESH,
        ),
        pltpu.make_async_remote_copy(
            factor_middle.at[group, pl.ds(0, rows)], factor_middle.at[group, pl.ds(0, rows)],
            factor_send_sem.at[1], factor_recv_sem.at[1],
            device_id=(over, sep), device_id_type=MESH,
        ),
    ]
    for copy in factor_copies:
        copy.start()

    def turn(which, turned):
        for part in range(2):
            at = pl.multiple_of(own_rank * (core if part == 0 else 1 - core), own_rank)
            turned[pl.ds(part * own_rank, own_rank), :] = couple_v[
                which, :, pl.ds(at, own_rank)
            ].T

    turn(0, turned_leaf)

    @pl.when(sep > 0)
    def _():
        to_next[0].wait_recv()

    @pl.when(sep < n_sep - 1)
    def _():
        to_prev[0].wait_recv()

    def solved(right_side, weight, before, after):
        scaled = right_side * weight
        up = jnp.where(row_at == 0, before, pltpu.roll(scaled, 1, 0))
        down = jnp.where(row_at == rows - 1, after, pltpu.roll(scaled, rows - 1, 0))
        return scaled + weight * (up + down)

    def place(i):
        here = lax.rem(i, 2)
        at_quarter = here * group + (1 - here) * (1 - group)
        return at_quarter * n_top + lax.div(i, 2)

    def to_device(src, dst, send_sem, recv_sem, dom_at, sep_at):
        return pltpu.make_async_remote_copy(
            src, dst, send_sem, recv_sem, device_id=(dom_at, sep_at), device_id_type=MESH
        )

    def pair_copy(slot):
        return to_device(
            pair_send.at[slot], pair_recv.at[slot], pair_send_sem.at[slot],
            pair_recv_sem.at[slot], front, sibling,
        )

    def right_copy(lines, first_slot, j):
        slot = first_slot + j
        return to_device(
            lines.at[0, j], lines.at[2, j], right_send_sem.at[slot],
            right_recv_sem.at[slot], front, sep + 2,
        )

    def left_copy(lines, first_slot, j):
        slot = first_slot + j
        return to_device(
            lines.at[1, j], lines.at[3, j], left_send_sem.at[slot],
            left_recv_sem.at[slot], front, sep - 2,
        )

    def final_copy(slot, coef, sem, child, i, dom_at, sep_at, lane):
        return to_device(
            final_send.at[slot],
            coef.at[child, i, pl.ds(pl.multiple_of(core * own_rank, own_rank), own_rank)],
            final_send_sem.at[slot, lax.rem(lane, 2)], sem.at[i, lane], dom_at, sep_at,
        )

    def start_pair(slot, turned, values):
        part = jnp.dot(turned[...], values, preferred_element_type=F32)
        own[slot] = part[:own_rank]
        pair_send[slot] = part[own_rank:]
        pair_copy(slot).start()

    def chain(t, count, base, first_slot, stride, lines, rank_now, coef, coef_sem, child, partner):
        def on(step, body):
            j = lax.div(step, stride) if stride > 1 else step
            hit = jnp.logical_and(step >= 0, step < stride * count)
            if stride > 1:
                hit = jnp.logical_and(hit, lax.rem(step, stride) == 0)

            @pl.when(hit)
            def _():
                body(j)

        def add_pair(j):
            slot = first_slot + j
            pair_copy(slot).wait_recv()
            own[slot] += pair_recv[slot]

        def prefix(j):
            slot = first_slot + j

            @pl.when(z > 0)
            def _():
                right_copy(lines, first_slot, j).wait_recv()

            @pl.when(z < n_z - 1)
            def _():
                lines[0, j] = (own[slot] + lines[2, j].astype(F32)).astype(lines.dtype)
                right_copy(lines, first_slot, j).start()

        def suffix(j):
            slot = first_slot + j

            @pl.when(z < n_z - 1)
            def _():
                left_copy(lines, first_slot, j).wait_recv()

            @pl.when(z > 0)
            def _():
                lines[1, j] = (own[slot] + lines[3, j].astype(F32)).astype(lines.dtype)
                left_copy(lines, first_slot, j).start()

        def final(j):
            slot = first_slot + j
            total = own[slot] + lines[2, j].astype(F32) + lines[3, j].astype(F32)
            at = core * own_rank + lax.broadcasted_iota(jnp.int32, total.shape, 0)
            kept = jnp.where(at < rank_now, total, 0.0).astype(BF16)
            final_send[slot] = kept
            i = lax.div(j, 2)

            @pl.when(lax.rem(j, 2) == 1)
            def _():
                coef[child, i, pl.ds(pl.multiple_of(core * own_rank, own_rank), own_rank)] = kept
                final_copy(slot, coef, coef_sem, child, i, front, sibling, 0).start()

            @pl.when(lax.rem(j, 2) == 0)
            def _():
                final_copy(slot, coef, coef_sem, child, i, partner, sep, 1).start()
                final_copy(slot, coef, coef_sem, child, i, partner, sibling, 2).start()

        start = t - base
        on(start, add_pair)
        on(start - z * HOP, prefix)
        on(start - (n_z - 1 - z) * HOP, suffix)
        on(start - jnp.maximum(z, n_z - 1 - z) * HOP, final)

    def await_coef(coef, sem, child, i):
        block = coef.at[child, i, pl.ds(0, own_rank)]
        for lane in range(3):
            to_device(
                final_send.at[0], block, final_send_sem.at[0, 0], sem.at[i, lane], front, sibling
            ).wait_recv()

    def applied(factor, coef, i):
        return jnp.dot(factor[0], coef[0, i], preferred_element_type=F32) + jnp.dot(
            factor[1], coef[1, i], preferred_element_type=F32
        )

    def leaf_step(j):
        i = lax.div(j, 2)
        own_side = lax.rem(j, 2)
        at_side = own_side * side + (1 - own_side) * (1 - side)
        at = pl.multiple_of(at_side * half + place(i) * CW, CW)
        values = solved(
            leaf_v[:, pl.ds(at, CW)].astype(F32), weights[0],
            edge_recv[0, :, pl.ds(at, CW)], edge_recv[1, :, pl.ds(at, CW)],
        ).astype(BF16)
        start_pair(j, turned_leaf, values)

    tail = width + half + quarter

    def eliminated(right_v, offset, at, factor, coef, i, which):
        taken = applied(factor, coef, i)
        beyond = []
        for way in range(2):
            right = edge_recv[way, :, pl.ds(pl.multiple_of(offset + at, CW), CW)]
            weight = edge_recv[way, :, tail + (which - 1) * CW : tail + which * CW]
            beyond.append((right - taken[rows + way : rows + way + 1]) * weight)
        return solved(
            right_v[:, pl.ds(at, CW)].astype(F32) - taken[:rows], weights[which], *beyond
        )

    def middle_step(i):
        await_coef(coef_leaf, coef_leaf_sem, side, i)
        at = pl.multiple_of(place(i) * CW, CW)
        values = eliminated(middle_v, width, at, factor_leaf, coef_leaf, i, 1).astype(BF16)
        start_pair(n_leaf + i, turned_middle, values)

    def top_step(i):
        await_coef(coef_middle, coef_middle_sem, group, i)
        at = pl.multiple_of(i * CW, CW)
        out[0, :, pl.ds(at, CW)] = eliminated(
            top_v, width + half, at, factor_middle, coef_middle, i, 2
        )

    def ready():
        loads[12].wait()
        turn(1, turned_middle)

        @pl.when(sep > 0)
        def _():
            for copy in to_next[1:]:
                copy.wait_recv()

        @pl.when(sep < n_sep - 1)
        def _():
            for copy in to_prev[1:]:
                copy.wait_recv()

        for copy in factor_copies:
            copy.wait_recv()

        at_row = lax.broadcasted_iota(jnp.int32, (16, rank), 0)

        def edge_tile(slot, lanes):
            before = row_recv[slot, 0, :, lanes]
            after = row_recv[slot, 1, :, lanes]
            tile = jnp.where(at_row == 0, before, jnp.where(at_row == 1, after, 0.0))
            return tile.astype(BF16)

        low, high = slice(0, rank), slice(rank, 2 * rank)
        factor_leaf[side, rows : rows + 16, :] = edge_tile(0, low)
        factor_leaf[1 - side, rows : rows + 16, :] = edge_tile(1, low)
        factor_middle[group, rows : rows + 16, :] = edge_tile(0, high)
        factor_middle[1 - group, rows : rows + 16, :] = edge_tile(2, high)

    leaf_base = LAG
    middle_at = leaf_base + (n_z - 1) * HOP + LAND + 1
    middle_base = middle_at + LAG
    top_at = middle_base + 2 + (n_z - 1) * HOP + LAND
    steps = top_at + 4 * (n_top - 1) + 1
    rank_leaf_now = rank_leaf[0]
    rank_middle_now = rank_middle[front // 2]

    def step(t, carry):
        @pl.when(t < n_leaf)
        def _():
            leaf_step(t)

        @pl.when(t == n_leaf)
        def _():
            ready()

        @pl.when(t < leaf_base + n_leaf + (n_z - 1) * HOP)
        def _():
            chain(
                t, n_leaf, leaf_base, 0, 1, leaf_lines, rank_leaf_now, coef_leaf, coef_leaf_sem,
                side, across,
            )

        i_mid = t - middle_at

        @pl.when(
            jnp.logical_and(i_mid >= 0, jnp.logical_and(i_mid < 2 * n_mid, lax.rem(i_mid, 2) == 0))
        )
        def _():
            middle_step(lax.div(i_mid, 2))

        @pl.when(t >= middle_base)
        def _():
            chain(
                t, n_mid, middle_base, n_leaf, 2, middle_lines, rank_middle_now, coef_middle,
                coef_middle_sem, group, over,
            )

        i_top = t - top_at

        @pl.when(jnp.logical_and(i_top >= 0, lax.rem(i_top, 4) == 0))
        def _():
            top_step(lax.div(i_top, 4))

        return carry

    lax.fori_loop(0, steps, step, 0)

    @pl.when(sep < n_sep - 1)
    def _():
        for copy in to_next:
            copy.wait_send()

    @pl.when(sep > 0)
    def _():
        for copy in to_prev:
            copy.wait_send()

    for copy in factor_copies:
        copy.wait_send()

    def drain(lines, first_slot, j, carry):
        slot = first_slot + j
        pair_copy(slot).wait_send()

        @pl.when(z < n_z - 1)
        def _():
            right_copy(lines, first_slot, j).wait_send()

        @pl.when(z > 0)
        def _():
            left_copy(lines, first_slot, j).wait_send()

        final_copy(slot, coef_leaf, coef_leaf_sem, side, 0, front, sibling, 0).wait_send()

        @pl.when(lax.rem(j, 2) == 0)
        def _():
            final_copy(slot, coef_leaf, coef_leaf_sem, side, 0, across, sep, 1).wait_send()

        return carry

    lax.fori_loop(0, n_leaf, functools.partial(drain, leaf_lines, 0), 0)
    lax.fori_loop(0, n_mid, functools.partial(drain, middle_lines, n_leaf), 0)


def shards(*operands):
    n_sep = lax.axis_size("sep")
    rows, width = operands[0].shape[1:]
    rank = operands[3].shape[2]
    half, quarter = width // 2, width // 4
    own_rank = rank // 2
    n_top = quarter // CW
    n_mid = 2 * n_top
    slots = 3 * n_mid
    chunk = (slots, own_rank, CW)
    tail = width + half + quarter + 2 * CW
    dma = pltpu.SemaphoreType.DMA
    hbm = pl.BlockSpec(memory_space=pltpu.HBM)
    vmem = pl.BlockSpec(memory_space=pltpu.VMEM)
    return pl.pallas_call(
        functools.partial(kernel, n_sep),
        out_shape=jax.ShapeDtypeStruct((1, rows, quarter), F32),
        in_specs=[hbm] * 13,
        out_specs=vmem,
        scratch_shapes=[
            pltpu.SMEM(operands[10].shape, jnp.int32),
            pltpu.SMEM(operands[11].shape, jnp.int32),
            pltpu.SMEM(operands[12].shape, jnp.int32),
            pltpu.VMEM((3, 1, rows), F32),
            pltpu.VMEM((rows, width), BF16),
            pltpu.VMEM((rows, half), BF16),
            pltpu.VMEM((rows, quarter), BF16),
            pltpu.VMEM((2, rows, rank), BF16),
            pltpu.VMEM((2, rows + 16, rank), BF16),
            pltpu.VMEM((2, rows + 16, rank), BF16),
            pltpu.VMEM((rank, rows), BF16),
            pltpu.VMEM((rank, rows), BF16),
            pltpu.VMEM((3, rows, CW), F32),
            pltpu.VMEM((2, 1, tail), F32),
            pltpu.VMEM((2, 1, tail), F32),
            pltpu.VMEM((2, 1, 2 * rank), F32),
            pltpu.VMEM((3, 2, 1, 2 * rank), F32),
            pltpu.VMEM(chunk, F32),
            pltpu.VMEM(chunk, F32),
            pltpu.VMEM(chunk, F32),
            pltpu.VMEM((4, 2 * n_mid, own_rank, CW), BF16),
            pltpu.VMEM((4, n_mid, own_rank, CW), F32),
            pltpu.VMEM(chunk, BF16),
            pltpu.VMEM((2, n_mid, rank, CW), BF16),
            pltpu.VMEM((2, n_top, rank, CW), BF16),
            dma((13,)),
            dma((2,)),
            dma((2,)),
            dma((2,)),
            dma((2,)),
            dma((3, 2)),
            dma((3, 2)),
            dma((slots,)),
            dma((slots,)),
            dma((slots,)),
            dma((slots,)),
            dma((slots,)),
            dma((slots,)),
            dma((slots, 2)),
            dma((n_mid, 3)),
            dma((n_top, 3)),
        ],
        compiler_params=pltpu.CompilerParams(
            collective_id=0, has_side_effects=True, vmem_limit_bytes=67043328
        ),
    )(*operands)


def solution(mesh):
    return jax.shard_map(
        shards,
        mesh=mesh,
        in_specs=(
            P("dom", "sep", None),
            P("dom", "sep", None),
            P("dom", "sep", None),
            P("dom", "sep", None),
            P("dom", "sep", None),
            P("dom", "sep", None),
            P("dom", "sep", None),
            P("dom", "sep"),
            P(None, "sep"),
            P(None, "sep"),
            P("dom", "sep"),
            P("dom"),
            P(),
        ),
        out_specs=P("dom", "sep", None),
        check_vma=False,
    )
```
